1024 devices in a mesh: seq: 64 (over z_lo, y, core), chan: 16 (over z_hi, x).
Axes of the slice: x: 4, y: 4, z: 32 (z_hi: 4, z_lo: 8; z = z_hi * 8 + z_lo), core: 2. Of those that a mesh axis runs over, the one named last changes fastest.
Arguments:
- out_grads: bfloat16 [8192, 4096], P(('seq', 'chan')), may hold values from -6 to 6
- layer_inputs: bfloat16 [8192, 4096], P('seq', 'chan'), may hold values from -0.015625 to 0.015625
- filters: bfloat16 [512, 256], P('seq', 'chan'), may hold values from -0.25 to 0.25
Outputs:
- input_grads: bfloat16 [8192, 4096], P('seq', 'chan')
- filter_grads: float32 [512, 256], P('seq', 'chan')
The draws below stay inside these ranges and needn't reach their ends.
All inputs are finite; a program needn't handle non-finite values.
Results may differ from the reference program's by a relative error of at most 0.001.
Values may be sent and summed in bfloat16 or wider, within the bound.
A program may use at most 32 MiB of HBM per device.

```python
import jax
import jax.numpy as jnp
from jax import lax

D = 4096
GROUPS = 256
BLOCK = 128
REACH = 4
TAPS = 512
SEQ = 8192
N_SEQ = 64


def block_scale(own_key, dims, cuts, least, high):
    def one(dim, parts):
        draws = jax.random.uniform(jax.random.fold_in(jax.random.fold_in(own_key, 6), dim), (parts,), jnp.float32, least / len(cuts), high / len(cuts))
        return jnp.repeat(jnp.exp(draws), dims[dim] // parts).reshape((-1,) + (1,) * (len(dims) - dim - 1))

    level = one(*cuts[0])
    for cut in cuts[1:]:
        level = level * one(*cut)
    return level


def scatter_about(own_key, dims, deviation, limit, shards=(), held_as=jnp.bfloat16):
    level = block_scale(own_key, dims, shards, -0.22, 0.18) if shards else 1.0
    entries = jax.random.normal(own_key, dims, jnp.float32) * deviation * level
    return jnp.minimum(jnp.maximum(entries, -limit), limit).astype(held_as)


def setup_inputs(seed: int = 0) -> dict:
    arg_keys = jax.random.split(jax.random.key(seed), 4)
    return {
        "out_grads": scatter_about(arg_keys[0], (SEQ, D), 1.0, 6.0, ((0, 1024),)),
        "layer_inputs": scatter_about(arg_keys[1], (SEQ, D), (SEQ * (D // GROUPS)) ** -0.5, 0.015625, ((0, 64), (1, 16))),
        "filters": scatter_about(arg_keys[2], (TAPS, GROUPS), TAPS ** -0.5, 0.25, ((0, 64), (1, 16))),
    }


def diagonal_sums(products):
    groups_here, length, _ = products.shape
    flipped = products[:, ::-1, :]
    padded = jnp.pad(flipped, ((0, 0), (0, 0), (0, length)))
    flat = padded.reshape(groups_here, 2 * length * length)[:, : length * (2 * length - 1)]
    return flat.reshape(groups_here, length, 2 * length - 1).sum(axis=1)


def reference(out_grads, layer_inputs, filters):
    per_group = D // GROUPS
    filt_rows = filters.astype(jnp.float32).T
    grad_blocks = out_grads.astype(jnp.float32).reshape(N_SEQ, BLOCK, GROUPS, per_group)
    input_blocks = layer_inputs.astype(jnp.float32).reshape(N_SEQ, BLOCK, GROUPS, per_group)
    offsets = jnp.arange(BLOCK, dtype=jnp.int32)[None, :] - jnp.arange(BLOCK, dtype=jnp.int32)[:, None]

    def one_block(index):
        x_block = input_blocks[index]
        dx_total = jnp.zeros((BLOCK, GROUPS, per_group), jnp.float32)
        lag_buffer = jnp.zeros((GROUPS, (REACH + 2) * BLOCK), jnp.float32)
        for lag_block in range(REACH + 1):
            current = grad_blocks[jnp.mod(index + lag_block, N_SEQ)]
            lag_index = lag_block * BLOCK + offsets
            inside = (lag_index >= 0) & (lag_index < TAPS)
            toeplitz = jnp.where(inside[None], filt_rows[:, jnp.clip(lag_index, 0, TAPS - 1)], jnp.float32(0.0))
            dx_total = dx_total + jnp.einsum("guv,vgk->ugk", toeplitz, current, precision=lax.Precision.HIGHEST)
            products = jnp.einsum("vgk,ugk->guv", current, x_block, precision=lax.Precision.HIGHEST)
            start = lag_block * BLOCK
            lag_buffer = lag_buffer.at[:, start:start + 2 * BLOCK - 1].add(diagonal_sums(products))
        return dx_total, lag_buffer[:, BLOCK - 1:BLOCK - 1 + TAPS]

    dx_blocks, dh_blocks = lax.map(one_block, jnp.arange(N_SEQ, dtype=jnp.int32))
    input_grads = dx_blocks.reshape(SEQ, D).astype(jnp.bfloat16)
    filter_grads = jnp.sum(dh_blocks, axis=0).T
    return input_grads, filter_grads
```

```python
import functools

import jax
import jax.numpy as jnp
from jax import lax
from jax.experimental import pallas as pl
from jax.experimental.pallas import tpu as pltpu
from jax.sharding import PartitionSpec as P

MESH = pl.DeviceIdType.MESH
LANES = 128
INNER = 8
CROSS = 4
GANG = 4


def kernel(ns, nc, dy_hbm, x_hbm, filt_ref, dx_hbm, dh_ref,
           dy_buf, dyc, x_buf, x_rev, row_buf, tile_buf, gathered, unpacked, frow, toep, dh_rows, dh_cols,
           packed, rs1, mid, rs2, dx_buf,
           s_a2a, r_a2a, s_row, r_row, s_tile, r_tile, s_halo, r_halo, s_rs1, r_rs1, s_rs2, r_rs2, s_loc):
    f32, bf16 = jnp.float32, jnp.bfloat16
    outer, zs = ns // INNER, nc // CROSS
    rows, width = dy_buf.shape[2], dy_buf.shape[3]
    block = rows * nc
    reach = dy_buf.shape[0] - 1
    span = (reach + 1) * block
    taps = reach * block
    groups = filt_ref.shape[1]
    per = width // groups
    s, c = lax.axis_index("seq"), lax.axis_index("chan")
    zo, yc = s // INNER, lax.rem(s, INNER)
    zh, xx = c // CROSS, lax.rem(c, CROSS)

    def chan_peer(dz, dx):
        return lax.rem(zh + dz, zs) * CROSS + lax.rem(xx + dx, CROSS)

    def inner_peer(j):
        return zo * INNER + lax.rem(yc + j, INNER)

    def outer_peer(j):
        return lax.rem(zo + j, outer) * INNER + yc

    def send(src, dst, ssem, rsem, seq, chan):
        copy = pltpu.make_async_remote_copy(
            src_ref=src, dst_ref=dst, send_sem=ssem, recv_sem=rsem, device_id=(seq, chan), device_id_type=MESH)
        copy.start()
        return copy

    hops = [(dz, dx) for dz in sorted(range(zs), key=lambda d: -min(d, zs - d)) for dx in range(CROSS) if dz or dx]
    order = sorted(range(zs), key=lambda d: min(d, zs - d))

    barrier = pltpu.get_barrier_semaphore()
    friends = [(s, chan_peer(dz, dx)) for dz, dx in hops]
    friends += [(inner_peer(j), c) for j in range(1, INNER)]
    friends += [(outer_peer(j), c) for j in range(1, outer)]
    for k in range(1, reach + 1):
        friends += [(lax.rem(s + k, ns), c), (lax.rem(s + ns - k, ns), c)]
    for friend in friends:
        pl.semaphore_signal(barrier, inc=1, device_id=friend, device_id_type=MESH)

    own = pltpu.make_async_copy(
        dy_hbm.at[:, pl.ds(pl.multiple_of(c * width, width), width)], dy_buf.at[0, c], s_loc.at[0])
    own.start()
    x_in = pltpu.make_async_copy(x_hbm, x_buf, s_loc.at[1])
    x_in.start()

    unpacked[...] = jnp.zeros_like(unpacked)
    unpacked[0:8, 0:groups] = filt_ref[...].astype(f32)
    flat = jnp.sum(pltpu.roll(unpacked[0:8, :], 0, 1, stride=groups, stride_axis=0), axis=0, keepdims=True)
    row_buf[yc] = flat

    pl.semaphore_wait(barrier, len(friends))

    sent = []
    for dz, dx in hops:
        peer = chan_peer(dz, dx)
        sent.append(send(dy_hbm.at[:, pl.ds(pl.multiple_of(peer * width, width), width)], dy_buf.at[0, c],
                         s_a2a.at[dz, dx], r_a2a.at[dz, dx], s, peer))
    row_sends = [send(row_buf.at[yc], row_buf.at[yc], s_row.at[j], r_row.at[j], inner_peer(j), c)
                 for j in range(1, INNER)]
    for copy in row_sends:
        copy.wait()
    for i in range(INNER):
        tile_buf[zo, i:i + 1, :] = row_buf[i]
    tile_sends = [send(tile_buf.at[zo], tile_buf.at[zo], s_tile.at[j], r_tile.at[j], outer_peer(j), c)
                  for j in range(1, outer)]

    own.wait()
    a2a = dict(zip(hops, sent))
    halo = []
    for dz in order:
        for dx in range(CROSS):
            if dz or dx:
                a2a[dz, dx].wait()
        first = lax.rem(zh + zs - dz, zs) * CROSS
        for k in range(1, reach + 1):
            halo.append(send(dy_buf.at[0, pl.ds(first, CROSS)], dy_buf.at[k, pl.ds(first, CROSS)],
                             s_halo.at[k - 1, dz], r_halo.at[k - 1, dz], lax.rem(s + ns - k, ns), c))

    x_in.wait()
    r0 = lax.broadcasted_iota(jnp.int32, (block, block), 0)
    r1 = lax.broadcasted_iota(jnp.int32, (block, block), 1)
    flip = jnp.where(r0 + r1 == block - 1, 1.0, 0.0).astype(bf16)
    x_rev[...] = jnp.dot(flip, x_buf[...], preferred_element_type=f32).astype(bf16)

    for copy in tile_sends:
        copy.wait()
    gathered[...] = tile_buf[...].reshape(outer * INNER, LANES)
    for t in range(8):
        turned = gathered[...] if t == 0 else pltpu.roll(gathered[...], LANES - t * groups, 1)
        unpacked[pl.ds(t, taps // 8, stride=8), :] = turned
    frow[...] = jnp.zeros_like(frow)
    for b in range(taps // LANES):
        frow[:, b * LANES:(b + 1) * LANES] = unpacked[b * LANES:(b + 1) * LANES, :].T[0:groups, :]

    def build(g, _):
        wide = jnp.broadcast_to(frow[pl.ds(g, 1), :], (block, span))
        toep[g] = pltpu.roll(wide, 0, 1, stride=1, stride_axis=0).astype(bf16)
        return 0

    lax.fori_loop(0, groups, build, 0)

    for copy in halo:
        copy.wait()
    for k in range(reach + 1):
        dyc[k * block:(k + 1) * block, :] = dy_buf[k].astype(f32).reshape(block, width).astype(bf16)

    lane_group = lax.broadcasted_iota(jnp.int32, (block, width), 1) // per
    dh_rows[...] = jnp.zeros_like(dh_rows)

    def correlate(i, _):
        xr = x_rev[...]
        masked = jnp.concatenate(
            [jnp.where(lane_group == i * GANG + q, xr, jnp.zeros_like(xr)) for q in range(GANG)], axis=0)
        products = lax.dot_general(masked, dyc[...], (((1,), (1,)), ((), ())), preferred_element_type=f32)
        for q in range(GANG):
            skewed = pltpu.roll(products[q * block:(q + 1) * block, :], 0, 1, stride=1, stride_axis=0)
            dh_rows[pl.ds(i * GANG + q, 1), :] = jnp.sum(skewed, axis=0, keepdims=True)
        return 0

    lax.fori_loop(0, groups // GANG, correlate, 0)
    aligned = pltpu.roll(dh_rows[...], span - (block - 1), 1)
    for b in range(taps // LANES):
        dh_cols[b * LANES:(b + 1) * LANES, :] = aligned[:, b * LANES:(b + 1) * LANES].T
    rows_packed = dh_cols[pl.ds(0, taps // 8, stride=8), :]
    for t in range(1, 8):
        rows_packed = rows_packed + pltpu.roll(dh_cols[pl.ds(t, taps // 8, stride=8), :], t * groups, 1)
    packed[...] = rows_packed.reshape(outer, INNER, LANES)
    rs1[0] = packed[zo]
    rs1_sends = []
    for j in range(1, outer):
        peer = lax.rem(zo + j, outer)
        rs1_sends.append(send(packed.at[peer], rs1.at[j], s_rs1.at[j], r_rs1.at[j], peer * INNER + yc, c))

    def convolve(i, acc):
        filters = toep[pl.ds(i * GANG, GANG)].reshape(GANG * block, span)
        out = jnp.dot(filters, dyc[...], preferred_element_type=f32)
        for q in range(GANG):
            acc = jnp.where(lane_group == i * GANG + q, out[q * block:(q + 1) * block, :], acc)
        return acc

    dx_buf[...] = lax.fori_loop(0, groups // GANG, convolve, jnp.zeros((block, width), f32)).astype(bf16)
    dx_out = pltpu.make_async_copy(dx_buf, dx_hbm, s_loc.at[2])
    dx_out.start()

    for copy in rs1_sends:
        copy.wait()
    mid[...] = jnp.sum(rs1[...], axis=0)
    rs2_sends = [send(mid, rs2.at[j], s_rs2.at[j], r_rs2.at[j], inner_peer(j), c) for j in range(1, INNER)]
    rs2[0] = mid[...]
    for copy in rs2_sends:
        copy.wait()
    mine = rs2[0, pl.ds(yc, 1), :]
    for j in range(1, INNER):
        mine = mine + rs2[j, pl.ds(yc, 1), :]
    for t in range(8):
        dh_ref[t:t + 1, :] = mine[:, t * groups:(t + 1) * groups]
    dx_out.wait()


def on_device(ns, nc, dy, x, filt):
    rows, width = dy.shape[0], x.shape[1]
    block = x.shape[0]
    groups = filt.shape[1]
    taps = filt.shape[0] * ns
    reach = taps // block
    span = taps + block
    outer, zs = ns // INNER, nc // CROSS
    f32, bf16 = jnp.float32, jnp.bfloat16
    vmem, dma = pltpu.VMEM, pltpu.SemaphoreType.DMA
    return pl.pallas_call(
        functools.partial(kernel, ns, nc),
        out_shape=(jax.ShapeDtypeStruct(x.shape, bf16), jax.ShapeDtypeStruct(filt.shape, f32)),
        in_specs=[pl.BlockSpec(memory_space=pl.ANY), pl.BlockSpec(memory_space=pl.ANY),
                  pl.BlockSpec(memory_space=pltpu.VMEM)],
        out_specs=(pl.BlockSpec(memory_space=pl.ANY), pl.BlockSpec(memory_space=pltpu.VMEM)),
        scratch_shapes=[
            vmem((reach + 1, nc, rows, width), bf16),
            vmem((span, width), bf16),
            vmem((block, width), bf16),
            vmem((block, width), bf16),
            vmem((INNER, 1, LANES), f32),
            vmem((outer, INNER, LANES), f32),
            vmem((ns, LANES), f32),
            vmem((taps, LANES), f32),
            vmem((groups, span), f32),
            vmem((groups, block, span), bf16),
            vmem((LANES, span), f32),
            vmem((taps, LANES), f32),
            vmem((outer, INNER, LANES), f32),
            vmem((outer, INNER, LANES), f32),
            vmem((INNER, LANES), f32),
            vmem((INNER, INNER, LANES), f32),
            vmem((block, width), bf16),
            dma((zs, CROSS)), dma((zs, CROSS)),
            dma((INNER,)), dma((INNER,)),
            dma((outer,)), dma((outer,)),
            dma((reach, zs)), dma((reach, zs)),
            dma((outer,)), dma((outer,)),
            dma((INNER,)), dma((INNER,)),
            dma((3,)),
        ],
        compiler_params=pltpu.CompilerParams(
            collective_id=0, has_side_effects=True, vmem_limit_bytes=40 * 2**20),
    )(dy, x, filt)


def solution(mesh):
    ns, nc = mesh.shape["seq"], mesh.shape["chan"]
    in_specs = (P(("seq", "chan"), None), P("seq", "chan"), P("seq", "chan"))
    out_specs = (P("seq", "chan"), P("seq", "chan"))
    return jax.shard_map(
        functools.partial(on_device, ns, nc), mesh=mesh, in_specs=in_specs, out_specs=out_specs, check_vma=False)
```

```python
import functools

import jax
import jax.numpy as jnp
from jax import lax
from jax.experimental import pallas as pl
from jax.experimental.pallas import tpu as pltpu
from jax.sharding import PartitionSpec as P

MESH = pl.DeviceIdType.MESH
LANES = 128
CROSS = 4
GANG = 4


def kernel(ns, nc, dy_hbm, x_hbm, filt_ref, dx_hbm, dh_ref,
           dy_buf, dyc, x_buf, x_half, x_ext, xw, row_buf, gathered, unpacked, frow, toep, dh_rows, dh_cols,
           staged, packed, rs, dx_out, dx_buf,
           s_a2a, r_a2a, s_x, r_x, s_row, r_row, s_halo, r_halo, s_rs, r_rs, s_dx, r_dx, s_loc):
    f32, bf16 = jnp.float32, jnp.bfloat16
    zs = nc // CROSS
    rows, half = dy_buf.shape[2], dy_buf.shape[3]
    block = rows * nc
    width = 2 * half
    quarter = block // zs
    span = dyc.shape[0]
    reach = span // block - 1
    taps = reach * block
    groups = filt_ref.shape[1]
    per = width // groups
    mine = groups // 2
    s, c = lax.axis_index("seq"), lax.axis_index("chan")
    e = lax.rem(s, 2)
    sib = s + 1 - 2 * e
    zh, xx = c // CROSS, lax.rem(c, CROSS)

    def chan_peer(dz, dx):
        return lax.rem(zh + dz, zs) * CROSS + lax.rem(xx + dx, CROSS)

    def copy_to(src, dst, ssem, rsem, seq, chan):
        return pltpu.make_async_remote_copy(
            src_ref=src, dst_ref=dst, send_sem=ssem, recv_sem=rsem, device_id=(seq, chan), device_id_type=MESH)

    def send(*args):
        copy = copy_to(*args)
        copy.start()
        return copy

    far = sorted(range(zs), key=lambda d: -min(d, zs - d))
    near = far[::-1]
    cores = ((0, s), (1, sib))

    barrier = pltpu.get_barrier_semaphore()
    friends = [(seq, chan_peer(dz, dx)) for dz in far for dx in range(CROSS) for _, seq in cores if dz or dx]
    for friend in friends:
        pl.semaphore_signal(barrier, inc=1, device_id=friend, device_id_type=MESH)

    def greet(j, _):
        pl.semaphore_signal(barrier, inc=1, device_id=(lax.rem(s + j, ns), c), device_id_type=MESH)
        return 0

    lax.fori_loop(1, ns, greet, 0)

    x_in = pltpu.make_async_copy(x_hbm, x_buf, s_loc.at[1])
    x_in.start()
    own = pltpu.make_async_copy(
        dy_hbm.at[:, pl.ds(pl.multiple_of(c * width + e * half, half), half)], dy_buf.at[e, c], s_loc.at[0])
    own.start()

    unpacked[...] = jnp.zeros_like(unpacked)
    unpacked[0:8, 0:groups] = filt_ref[...].astype(f32)
    row_buf[s] = jnp.sum(pltpu.roll(unpacked[0:8, :], 0, 1, stride=groups, stride_axis=0), axis=0, keepdims=True)
    frow[...] = jnp.zeros_like(frow)
    dh_rows[...] = jnp.zeros_like(dh_rows)

    x_in.wait()
    r0 = lax.broadcasted_iota(jnp.int32, (block, block), 0)
    r1 = lax.broadcasted_iota(jnp.int32, (block, block), 1)
    flip = jnp.where(r0 + r1 == block - 1, 1.0, 0.0).astype(bf16)
    for h in range(2):
        x_half[h] = jnp.dot(flip, x_buf[:, h * half:(h + 1) * half], preferred_element_type=f32).astype(bf16)
    x_ext[1 - e] = x_half[e]

    pl.semaphore_wait(barrier, len(friends) + ns - 1)

    a2a = {}
    for dz in far:
        for dx in range(CROSS):
            for r, seq in cores:
                if dz or dx or r:
                    peer = chan_peer(dz, dx)
                    their = e if r == 0 else 1 - e
                    start = pl.multiple_of(peer * width + their * half, half)
                    a2a[dz, dx, r] = send(dy_hbm.at[:, pl.ds(start, half)], dy_buf.at[e, c],
                                          s_a2a.at[dz, dx, r], r_a2a.at[dz, dx, r], seq, peer)
    x_sends = []
    for m in range(reach // 2 + 1):
        for r, seq in cores:
            if m or r:
                their = e if r == 0 else 1 - e
                x_sends.append(send(x_half.at[their], x_ext.at[2 * m + 1 - e],
                                    s_x.at[m, r], r_x.at[m, r], lax.rem(seq + 2 * m, ns), c))

    def send_row(j, _):
        copy_to(row_buf.at[s], row_buf.at[s], s_row, r_row, lax.rem(s + j, ns), c).start()
        return 0

    lax.fori_loop(1, ns, send_row, 0)
    all_rows = copy_to(row_buf.at[pl.ds(0, ns - 1)], row_buf.at[pl.ds(0, ns - 1)], s_row, r_row, sib, c)

    lane = lax.broadcasted_iota(jnp.int32, (quarter, width), 1)
    lane_group = lax.rem(lane, half) // per
    own.wait()
    halo = []
    total = jnp.zeros((mine, span), f32)
    for dz in near:
        for dx in range(CROSS):
            for r, _ in cores:
                if dz or dx or r:
                    a2a[dz, dx, r].wait_recv()
        zg = lax.rem(zh + zs - dz, zs)
        part = (pl.ds(0, 2), pl.ds(zg * CROSS, CROSS))
        for m in range(1, reach // 2 + 1):
            halo.append(send(dy_buf.at[part], dy_buf.at[pl.ds(2 * m, 2), pl.ds(zg * CROSS, CROSS)],
                             s_halo.at[m - 1, dz], r_halo.at[m - 1, dz], lax.rem(s + ns - 2 * m, ns), c))
        if dz == 0:
            for copy in x_sends:
                copy.wait_recv()
            for i in range(reach + 1):
                xw[i * block:(i + 1) * block, 0:half] = x_ext[i + 1]
                xw[i * block:(i + 1) * block, half:width] = x_ext[i]
        at = pl.ds(pl.multiple_of(zg * quarter, quarter), quarter)
        for b in range(2):
            chunk = dy_buf[b, pl.ds(zg * CROSS, CROSS)].astype(f32).reshape(quarter, half).astype(bf16)
            dyc[at, b * half:(b + 1) * half] = chunk
        grads = dyc[at, :]
        masked = jnp.concatenate(
            [jnp.where(lane_group == q, grads, jnp.zeros_like(grads)) for q in range(mine)], axis=0)
        products = lax.dot_general(masked, xw[...], (((1,), (1,)), ((), ())), preferred_element_type=f32)
        sums = []
        for q in range(mine):
            skewed = pltpu.roll(products[q * quarter:(q + 1) * quarter, :], 0, 1, stride=1, stride_axis=0)
            sums.append(jnp.sum(skewed, axis=0, keepdims=True))
        total = total + pltpu.roll(jnp.concatenate(sums, axis=0), zg * quarter, 1)

    dh_rows[pl.ds(pl.multiple_of(e * mine, mine), mine), :] = pltpu.roll(total, span - (block - 1), 1)
    for b in range(taps // LANES):
        dh_cols[b * LANES:(b + 1) * LANES, :] = dh_rows[:, b * LANES:(b + 1) * LANES].T
    rows_packed = dh_cols[pl.ds(0, ns, stride=8), :]
    for t in range(1, 8):
        rows_packed = rows_packed + pltpu.roll(dh_cols[pl.ds(t, ns, stride=8), :], t * groups, 1)
    staged[...] = rows_packed
    for i in range(ns):
        packed[i] = staged[i:i + 1, :]

    def send_terms(j, _):
        peer = lax.rem(s + j, ns)
        copy_to(packed.at[peer], rs.at[j], s_rs, r_rs, peer, c).start()
        return 0

    lax.fori_loop(1, ns, send_terms, 0)
    rs[0] = packed[s]
    all_terms = copy_to(packed.at[pl.ds(0, ns - 1)], rs.at[pl.ds(1, ns - 1)], s_rs, r_rs, sib, c)

    all_rows.wait_recv()
    for i in range(ns):
        gathered[i:i + 1, :] = row_buf[i]
    for t in range(8):
        turned = gathered[...] if t == 0 else pltpu.roll(gathered[...], LANES - t * groups, 1)
        unpacked[pl.ds(t, ns, stride=8), :] = turned
    for b in range(taps // LANES):
        frow[:, b * LANES:(b + 1) * LANES] = unpacked[b * LANES:(b + 1) * LANES, :].T[0:groups, :]

    def build(g, _):
        wide = jnp.broadcast_to(frow[pl.ds(e * mine + g, 1), :], (block, span))
        toep[g] = pltpu.roll(wide, 0, 1, stride=1, stride_axis=0).astype(bf16)
        return 0

    lax.fori_loop(0, mine, build, 0)

    for copy in halo:
        copy.wait_recv()
    for b in range(1, reach + 2):
        tile = dy_buf[b].astype(f32).reshape(block, half).astype(bf16)
        if b <= reach:
            dyc[b * block:(b + 1) * block, 0:half] = tile
        if b >= 2:
            dyc[(b - 1) * block:b * block, half:width] = tile

    lane_all = lax.rem(lax.broadcasted_iota(jnp.int32, (block, width), 1), half) // per

    def convolve(i, acc):
        filters = toep[pl.ds(i * GANG, GANG)].reshape(GANG * block, span)
        out = jnp.dot(filters, dyc[...], preferred_element_type=f32)
        for q in range(GANG):
            acc = jnp.where(lane_all == i * GANG + q, out[q * block:(q + 1) * block, :], acc)
        return acc

    grads_in = lax.fori_loop(0, mine // GANG, convolve, jnp.zeros((block, width), f32)).astype(bf16)
    for b in range(2):
        dx_out[b] = grads_in[:, b * half:(b + 1) * half]
    swap = send(dx_out.at[1 - e], dx_buf.at[e], s_dx, r_dx, sib, c)
    at = pl.ds(pl.multiple_of(e * half, half), half)
    kept = pltpu.make_async_copy(dx_out.at[e], dx_hbm.at[:, at], s_loc.at[2])
    kept.start()
    swap.wait_recv()
    at = pl.ds(pl.multiple_of((1 - e) * half, half), half)
    other = pltpu.make_async_copy(dx_buf.at[1 - e], dx_hbm.at[:, at], s_loc.at[3])
    other.start()

    all_terms.wait_recv()
    terms = jnp.sum(rs[...], axis=0)
    for t in range(8):
        dh_ref[t:t + 1, :] = terms[:, t * groups:(t + 1) * groups]

    kept.wait()
    other.wait()
    for copy in [*a2a.values(), *x_sends, *halo, all_rows, all_terms, swap]:
        copy.wait_send()


def on_device(ns, nc, dy, x, filt):
    rows = dy.shape[0]
    block, width = x.shape
    half = width // 2
    groups = filt.shape[1]
    taps = filt.shape[0] * ns
    reach = taps // block
    span = taps + block
    zs = nc // CROSS
    f32, bf16 = jnp.float32, jnp.bfloat16
    vmem, dma = pltpu.VMEM, pltpu.SemaphoreType.DMA
    return pl.pallas_call(
        functools.partial(kernel, ns, nc),
        out_shape=(jax.ShapeDtypeStruct(x.shape, bf16), jax.ShapeDtypeStruct(filt.shape, f32)),
        in_specs=[pl.BlockSpec(memory_space=pl.ANY), pl.BlockSpec(memory_space=pl.ANY),
                  pl.BlockSpec(memory_space=pltpu.VMEM)],
        out_specs=(pl.BlockSpec(memory_space=pl.ANY), pl.BlockSpec(memory_space=pltpu.VMEM)),
        scratch_shapes=[
            vmem((reach + 2, nc, rows, half), bf16),
            vmem((span, width), bf16),
            vmem((block, width), bf16),
            vmem((2, block, half), bf16),
            vmem((reach + 2, block, half), bf16),
            vmem((span, width), bf16),
            vmem((ns, 1, LANES), f32),
            vmem((ns, LANES), f32),
            vmem((taps, LANES), f32),
            vmem((groups, span), f32),
            vmem((groups // 2, block, span), bf16),
            vmem((LANES, span), f32),
            vmem((taps, LANES), f32),
            vmem((ns, LANES), f32),
            vmem((ns, 1, LANES), f32),
            vmem((ns, 1, LANES), f32),
            vmem((2, block, half), bf16),
            vmem((2, block, half), bf16),
            dma((zs, CROSS, 2)), dma((zs, CROSS, 2)),
            dma((reach // 2 + 1, 2)), dma((reach // 2 + 1, 2)),
            dma, dma,
            dma((reach // 2, zs)), dma((reach // 2, zs)),
            dma, dma, dma, dma,
            dma((4,)),
        ],
        compiler_params=pltpu.CompilerParams(
            collective_id=0, has_side_effects=True, vmem_limit_bytes=40 * 2**20),
    )(dy, x, filt)


def solution(mesh):
    ns, nc = mesh.shape["seq"], mesh.shape["chan"]
    in_specs = (P(("seq", "chan"), None), P("seq", "chan"), P("seq", "chan"))
    out_specs = (P("seq", "chan"), P("seq", "chan"))
    return jax.shard_map(
        functools.partial(on_device, ns, nc), mesh=mesh, in_specs=in_specs, out_specs=out_specs, check_vma=False)
```

```python
import functools

import jax
import jax.numpy as jnp
from jax import lax
from jax.experimental import pallas as pl
from jax.experimental.pallas import tpu as pltpu
from jax.sharding import PartitionSpec as P

MESH = pl.DeviceIdType.MESH
LANES = 128
CROSS = 4
GANG = 4


def kernel(ns, nc, dy_hbm, x_hbm, filt_hbm, dx_hbm, dh_ref,
           filt_ref, dy_buf, dyc, x_buf, x_half, x_ext, xw, row_buf, gathered, unpacked, frow, toep, dh_rows, dh_cols,
           staged, packed, rs, dx_out, dx_buf,
           s_a2a, r_a2a, s_x, r_x, s_row, r_row, s_halo, r_halo, s_rs, r_rs, s_dx, r_dx, s_loc):
    f32, bf16 = jnp.float32, jnp.bfloat16
    zs = nc // CROSS
    rows, half = dy_buf.shape[2], dy_buf.shape[3]
    block = rows * nc
    width = 2 * half
    quarter = block // zs
    span = dyc.shape[0]
    reach = span // block - 1
    taps = reach * block
    groups = filt_ref.shape[1]
    per = width // groups
    mine = groups // 2
    s, c = lax.axis_index("seq"), lax.axis_index("chan")
    e = lax.rem(s, 2)
    sib = s + 1 - 2 * e
    zh, xx = c // CROSS, lax.rem(c, CROSS)

    def chan_peer(dz, dx):
        return lax.rem(zh + dz, zs) * CROSS + lax.rem(xx + dx, CROSS)

    def copy_to(src, dst, ssem, rsem, seq, chan):
        return pltpu.make_async_remote_copy(
            src_ref=src, dst_ref=dst, send_sem=ssem, recv_sem=rsem, device_id=(seq, chan), device_id_type=MESH)

    def send(*args):
        copy = copy_to(*args)
        copy.start()
        return copy

    far = sorted(range(zs), key=lambda d: -min(d, zs - d))
    near = sorted(range(zs), key=lambda d: min(d, zs - d))
    cores = ((0, s), (1, sib))

    barrier = pltpu.get_barrier_semaphore()

    def greet_all(dz):
        for dx in range(CROSS):
            for r, seq in cores:
                if dz or dx:
                    pl.semaphore_signal(barrier, inc=1, device_id=(seq, chan_peer(dz, dx)), device_id_type=MESH)

    for dz in far[:-1]:
        pl.when(zh + dz < zs)(functools.partial(greet_all, dz))
    greet_all(0)

    def greet(j, _):
        pl.semaphore_signal(barrier, inc=1, device_id=(lax.rem(s + j, ns), c), device_id_type=MESH)
        return 0

    lax.fori_loop(1, ns, greet, 0)

    x_in = pltpu.make_async_copy(x_hbm, x_buf, s_loc.at[1])
    x_in.start()
    filt_in = pltpu.make_async_copy(filt_hbm, filt_ref, s_loc.at[4])
    filt_in.start()
    own = pltpu.make_async_copy(
        dy_hbm.at[:, pl.ds(pl.multiple_of(c * width + e * half, half), half)], dy_buf.at[e, c], s_loc.at[0])
    own.start()

    unpacked[...] = jnp.zeros_like(unpacked)
    filt_in.wait()
    unpacked[0:8, 0:groups] = filt_ref[...].astype(f32)
    row_buf[s] = jnp.sum(pltpu.roll(unpacked[0:8, :], 0, 1, stride=groups, stride_axis=0), axis=0, keepdims=True)
    frow[...] = jnp.zeros_like(frow)
    dh_rows[...] = jnp.zeros_like(dh_rows)

    x_in.wait()
    r0 = lax.broadcasted_iota(jnp.int32, (block, block), 0)
    r1 = lax.broadcasted_iota(jnp.int32, (block, block), 1)
    flip = jnp.where(r0 + r1 == block - 1, 1.0, 0.0).astype(bf16)
    for h in range(2):
        x_half[h] = jnp.dot(flip, x_buf[:, h * half:(h + 1) * half], preferred_element_type=f32).astype(bf16)
    x_ext[1 - e] = x_half[e]

    pl.semaphore_wait(barrier, 2 * (CROSS - 1) + ns - 1 + 2 * CROSS * zh)

    def chunk_copy(dz, dx, r):
        peer = chan_peer(dz, dx)
        their = e if r == 0 else 1 - e
        start = pl.multiple_of(peer * width + their * half, half)
        return copy_to(dy_hbm.at[:, pl.ds(start, half)], dy_buf.at[e, c],
                       s_a2a.at[dz, dx, r], r_a2a.at[dz, dx, r], cores[r][1], peer)

    def wanted(dz):
        return [(dz, dx, r) for dx in range(CROSS) for r in range(2) if dz or dx or r]

    def send_chunks(dz):
        for key in wanted(dz):
            chunk_copy(*key).start()

    for dz in far[:-1]:
        pl.when(zh + dz >= zs)(functools.partial(send_chunks, dz))
    send_chunks(0)
    x_sends = []
    for m in range(reach // 2 + 1):
        for r, seq in cores:
            if m or r:
                their = e if r == 0 else 1 - e
                x_sends.append(send(x_half.at[their], x_ext.at[2 * m + 1 - e],
                                    s_x.at[m, r], r_x.at[m, r], lax.rem(seq + 2 * m, ns), c))


    def send_row(j, _):
        copy_to(row_buf.at[s], row_buf.at[s], s_row, r_row, lax.rem(s + j, ns), c).start()
        return 0

    lax.fori_loop(1, ns, send_row, 0)
    all_rows = copy_to(row_buf.at[pl.ds(0, ns - 1)], row_buf.at[pl.ds(0, ns - 1)], s_row, r_row, sib, c)

    lane = lax.broadcasted_iota(jnp.int32, (quarter, width), 1)
    lane_group = lax.rem(lane, half) // per
    own.wait()
    halo = []
    total = jnp.zeros((mine, span), f32)
    for dz in near:
        for key in wanted((zs - dz) % zs):
            chunk_copy(*key).wait_recv()
        zg = lax.rem(zh + dz, zs)
        part = (pl.ds(0, 2), pl.ds(zg * CROSS, CROSS))
        for m in range(1, reach // 2 + 1):
            halo.append(send(dy_buf.at[part], dy_buf.at[pl.ds(2 * m, 2), pl.ds(zg * CROSS, CROSS)],
                             s_halo.at[m - 1, dz], r_halo.at[m - 1, dz], lax.rem(s + ns - 2 * m, ns), c))
        if dz:
            pl.when(zh + dz < zs)(functools.partial(send_chunks, dz))
        else:
            for copy in x_sends:
                copy.wait_recv()
            for i in range(reach + 1):
                xw[i * block:(i + 1) * block, 0:half] = x_ext[i + 1]
                xw[i * block:(i + 1) * block, half:width] = x_ext[i]
        at = pl.ds(pl.multiple_of(zg * quarter, quarter), quarter)
        for b in range(2):
            chunk = dy_buf[b, pl.ds(zg * CROSS, CROSS)].astype(f32).reshape(quarter, half).astype(bf16)
            dyc[at, b * half:(b + 1) * half] = chunk
        grads = dyc[at, :]
        masked = jnp.concatenate(
            [jnp.where(lane_group == q, grads, jnp.zeros_like(grads)) for q in range(mine)], axis=0)
        products = lax.dot_general(masked, xw[...], (((1,), (1,)), ((), ())), preferred_element_type=f32)
        sums = []
        for q in range(mine):
            skewed = pltpu.roll(products[q * quarter:(q + 1) * quarter, :], 0, 1, stride=1, stride_axis=0)
            sums.append(jnp.sum(skewed, axis=0, keepdims=True))
        total = total + pltpu.roll(jnp.concatenate(sums, axis=0), zg * quarter, 1)

    dh_rows[pl.ds(pl.multiple_of(e * mine, mine), mine), :] = pltpu.roll(total, span - (block - 1), 1)
    for b in range(taps // LANES):
        dh_cols[b * LANES:(b + 1) * LANES, :] = dh_rows[:, b * LANES:(b + 1) * LANES].T
    rows_packed = dh_cols[pl.ds(0, ns, stride=8), :]
    for t in range(1, 8):
        rows_packed = rows_packed + pltpu.roll(dh_cols[pl.ds(t, ns, stride=8), :], t * groups, 1)
    staged[...] = rows_packed
    for i in range(ns):
        packed[i] = staged[i:i + 1, :]

    def send_terms(j, _):
        peer = lax.rem(s + j, ns)
        copy_to(packed.at[peer], rs.at[j], s_rs, r_rs, peer, c).start()
        return 0

    lax.fori_loop(1, ns, send_terms, 0)
    rs[0] = packed[s]
    all_terms = copy_to(packed.at[pl.ds(0, ns - 1)], rs.at[pl.ds(1, ns - 1)], s_rs, r_rs, sib, c)

    all_rows.wait_recv()
    for i in range(ns):
        gathered[i:i + 1, :] = row_buf[i]
    for t in range(8):
        turned = gathered[...] if t == 0 else pltpu.roll(gathered[...], LANES - t * groups, 1)
        unpacked[pl.ds(t, ns, stride=8), :] = turned
    for b in range(taps // LANES):
        frow[:, b * LANES:(b + 1) * LANES] = unpacked[b * LANES:(b + 1) * LANES, :].T[0:groups, :]

    def build(g, _):
        wide = jnp.broadcast_to(frow[pl.ds(e * mine + g, 1), :], (block, span))
        toep[g] = pltpu.roll(wide, 0, 1, stride=1, stride_axis=0).astype(bf16)
        return 0

    lax.fori_loop(0, mine, build, 0)

    for copy in halo:
        copy.wait_recv()
    for b in range(1, reach + 2):
        tile = dy_buf[b].astype(f32).reshape(block, half).astype(bf16)
        if b <= reach:
            dyc[b * block:(b + 1) * block, 0:half] = tile
        if b >= 2:
            dyc[(b - 1) * block:b * block, half:width] = tile

    lane_all = lax.rem(lax.broadcasted_iota(jnp.int32, (block, width), 1), half) // per

    def convolve(i, acc):
        filters = toep[pl.ds(i * GANG, GANG)].reshape(GANG * block, span)
        out = jnp.dot(filters, dyc[...], preferred_element_type=f32)
        for q in range(GANG):
            acc = jnp.where(lane_all == i * GANG + q, out[q * block:(q + 1) * block, :], acc)
        return acc

    grads_in = lax.fori_loop(0, mine // GANG, convolve, jnp.zeros((block, width), f32)).astype(bf16)
    for b in range(2):
        dx_out[b] = grads_in[:, b * half:(b + 1) * half]
    swap = send(dx_out.at[1 - e], dx_buf.at[e], s_dx, r_dx, sib, c)
    at = pl.ds(pl.multiple_of(e * half, half), half)
    kept = pltpu.make_async_copy(dx_out.at[e], dx_hbm.at[:, at], s_loc.at[2])
    kept.start()
    swap.wait_recv()
    at = pl.ds(pl.multiple_of((1 - e) * half, half), half)
    other = pltpu.make_async_copy(dx_buf.at[1 - e], dx_hbm.at[:, at], s_loc.at[3])
    other.start()

    all_terms.wait_recv()
    terms = jnp.sum(rs[...], axis=0)
    for t in range(8):
        dh_ref[t:t + 1, :] = terms[:, t * groups:(t + 1) * groups]

    kept.wait()
    other.wait()
    for dz in range(zs):
        for key in wanted(dz):
            chunk_copy(*key).wait_send()
    for copy in [*x_sends, *halo, all_rows, all_terms, swap]:
        copy.wait_send()


def on_device(ns, nc, dy, x, filt):
    rows = dy.shape[0]
    block, width = x.shape
    half = width // 2
    groups = filt.shape[1]
    taps = filt.shape[0] * ns
    reach = taps // block
    span = taps + block
    zs = nc // CROSS
    f32, bf16 = jnp.float32, jnp.bfloat16
    vmem, dma = pltpu.VMEM, pltpu.SemaphoreType.DMA
    return pl.pallas_call(
        functools.partial(kernel, ns, nc),
        out_shape=(jax.ShapeDtypeStruct(x.shape, bf16), jax.ShapeDtypeStruct(filt.shape, f32)),
        in_specs=[pl.BlockSpec(memory_space=pltpu.HBM)] * 3,
        out_specs=(pl.BlockSpec(memory_space=pl.ANY), pl.BlockSpec(memory_space=pltpu.VMEM)),
        scratch_shapes=[
            vmem(filt.shape, bf16),
            vmem((reach + 2, nc, rows, half), bf16),
            vmem((span, width), bf16),
            vmem((block, width), bf16),
            vmem((2, block, half), bf16),
            vmem((reach + 2, block, half), bf16),
            vmem((span, width), bf16),
            vmem((ns, 1, LANES), f32),
            vmem((ns, LANES), f32),
            vmem((taps, LANES), f32),
            vmem((groups, span), f32),
            vmem((groups // 2, block, span), bf16),
            vmem((LANES, span), f32),
            vmem((taps, LANES), f32),
            vmem((ns, LANES), f32),
            vmem((ns, 1, LANES), f32),
            vmem((ns, 1, LANES), f32),
            vmem((2, block, half), bf16),
            vmem((2, block, half), bf16),
            dma((zs, CROSS, 2)), dma((zs, CROSS, 2)),
            dma((reach // 2 + 1, 2)), dma((reach // 2 + 1, 2)),
            dma, dma,
            dma((reach // 2, zs)), dma((reach // 2, zs)),
            dma, dma, dma, dma,
            dma((5,)),
        ],
        compiler_params=pltpu.CompilerParams(
            collective_id=0, has_side_effects=True, vmem_limit_bytes=60 * 2**20),
    )(dy, x, filt)


def solution(mesh):
    ns, nc = mesh.shape["seq"], mesh.shape["chan"]
    in_specs = (P(("seq", "chan"), None), P("seq", "chan"), P("seq", "chan"))
    out_specs = (P("seq", "chan"), P("seq", "chan"))
    return jax.shard_map(
        functools.partial(on_device, ns, nc), mesh=mesh, in_specs=in_specs, out_specs=out_specs, check_vma=False)
```

```python
import functools

import jax
import jax.numpy as jnp
from jax import lax
from jax.experimental import pallas as pl
from jax.experimental.pallas import tpu as pltpu
from jax.sharding import PartitionSpec as P

MESH = pl.DeviceIdType.MESH
LANES = 128
INNER = 8
CROSS = 4
GANG = 4


def kernel(ns, nc, dy_hbm, x_hbm, filt_hbm, dx_hbm, dh_ref,
           filt_ref, dy_buf, dyc, x_buf, x_half, x_ext, xw, row_buf, gathered, unpacked, frow, toep, dh_rows, dh_cols,
           staged, packed, rs, dx_out, dx_buf, relayed,
           s_a2a, r_a2a, s_rel, r_rel, s_fwd, r_fwd, s_x, r_x, s_row, r_row, s_halo, r_halo, s_rs, r_rs, s_dx, r_dx, s_loc):
    f32, bf16 = jnp.float32, jnp.bfloat16
    zs = nc // CROSS
    rows, half = dy_buf.shape[2], dy_buf.shape[3]
    block = rows * nc
    width = 2 * half
    quarter = block // zs
    span = dyc.shape[0]
    reach = span // block - 1
    taps = reach * block
    groups = filt_ref.shape[1]
    per = width // groups
    mine = groups // 2
    s, c = lax.axis_index("seq"), lax.axis_index("chan")
    e = lax.rem(s, 2)
    sib = s + 1 - 2 * e
    outer, zo, yc = ns // INNER, s // INNER, lax.rem(s, INNER)
    zh, xx = c // CROSS, lax.rem(c, CROSS)

    def chan_peer(dz, dx):
        return lax.rem(zh + dz, zs) * CROSS + lax.rem(xx + dx, CROSS)

    def copy_to(src, dst, ssem, rsem, seq, chan):
        return pltpu.make_async_remote_copy(
            src_ref=src, dst_ref=dst, send_sem=ssem, recv_sem=rsem, device_id=(seq, chan), device_id_type=MESH)

    def send(*args):
        copy = copy_to(*args)
        copy.start()
        return copy

    far = sorted(range(zs), key=lambda d: -min(d, zs - d))
    near = sorted(range(zs), key=lambda d: min(d, zs - d))
    cores = ((0, s), (1, sib))

    barrier = pltpu.get_barrier_semaphore()

    def greet_all(dz):
        for dx in range(CROSS):
            for r, seq in cores:
                if dz or dx:
                    pl.semaphore_signal(barrier, inc=1, device_id=(seq, chan_peer(dz, dx)), device_id_type=MESH)

    for dz in far[:-1]:
        pl.when(zh + dz < zs)(functools.partial(greet_all, dz))
    greet_all(0)

    def greet(j, _):
        pl.semaphore_signal(barrier, inc=1, device_id=(j, c), device_id_type=MESH)
        return 0

    def greet_inner(j, _):
        return greet(zo * INNER + lax.rem(yc + j, INNER), 0)

    lax.fori_loop(0, zo * INNER, greet, 0)
    lax.fori_loop(1, INNER, greet_inner, 0)

    x_in = pltpu.make_async_copy(x_hbm, x_buf, s_loc.at[1])
    x_in.start()
    filt_in = pltpu.make_async_copy(filt_hbm, filt_ref, s_loc.at[4])
    filt_in.start()
    own = pltpu.make_async_copy(
        dy_hbm.at[:, pl.ds(pl.multiple_of(c * width + e * half, half), half)], dy_buf.at[e, c], s_loc.at[0])
    own.start()

    pl.semaphore_wait(barrier, 2 * (CROSS - 1) + INNER - 1 + INNER * (outer - 1 - zo) + 2 * CROSS * zh)

    def chunk_copy(dz, dx, r):
        peer = chan_peer(dz, dx)
        their = e if r == 0 else 1 - e
        start = pl.multiple_of(peer * width + their * half, half)
        return copy_to(dy_hbm.at[:, pl.ds(start, half)], dy_buf.at[e, c],
                       s_a2a.at[dz, dx, r], r_a2a.at[dz, dx, r], cores[r][1], peer)

    def wanted(dz):
        return [(dz, dx, r) for dx in range(CROSS) for r in range(2) if dz or dx or r]

    def send_chunks(dz):
        for key in wanted(dz):
            chunk_copy(*key).start()

    via = lax.rem(zs + 1 - zh, zs)

    def relay_copy(dx, r):
        column = lax.rem(xx + dx, CROSS)
        their = e if r == 0 else 1 - e
        start = pl.multiple_of(((zh + 2) * CROSS + column) * width + their * half, half)
        return copy_to(dy_hbm.at[:, pl.ds(start, half)], relayed.at[e, xx],
                       s_rel.at[dx, r], r_rel.at[dx, r], cores[r][1], via * CROSS + column)

    relays = [(dx, r) for dx in range(CROSS) for r in range(2)]

    def send_relays():
        for key in relays:
            relay_copy(*key).start()

    forward = copy_to(relayed, dy_buf.at[pl.ds(0, 2), pl.ds(via * CROSS, CROSS)], s_fwd, r_fwd,
                      s, (3 - zh) * CROSS + xx)

    def send_forward():
        for key in relays:
            relay_copy(*key).wait_recv()
        forward.start()

    for dz in range(1, zs):
        pl.when(zh + dz == zs)(functools.partial(send_chunks, dz))
    send_chunks(0)

    unpacked[...] = jnp.zeros_like(unpacked)
    filt_in.wait()
    unpacked[0:8, 0:groups] = filt_ref[...].astype(f32)
    row_buf[s] = jnp.sum(pltpu.roll(unpacked[0:8, :], 0, 1, stride=groups, stride_axis=0), axis=0, keepdims=True)
    frow[...] = jnp.zeros_like(frow)
    dh_rows[...] = jnp.zeros_like(dh_rows)

    x_in.wait()
    r0 = lax.broadcasted_iota(jnp.int32, (block, block), 0)
    r1 = lax.broadcasted_iota(jnp.int32, (block, block), 1)
    flip = jnp.where(r0 + r1 == block - 1, 1.0, 0.0).astype(bf16)
    for h in range(2):
        x_half[h] = jnp.dot(flip, x_buf[:, h * half:(h + 1) * half], preferred_element_type=f32).astype(bf16)
    x_ext[1 - e] = x_half[e]

    def x_copy(m, r):
        their = e if r == 0 else 1 - e
        return copy_to(x_half.at[their], x_ext.at[2 * m + 1 - e], s_x.at[m, r], r_x.at[m, r],
                       lax.rem(cores[r][1] + 2 * m, ns), c)

    def send_x(m):
        for r in range(2):
            x_copy(m, r).start()

    x_copy(0, 1).start()
    later = range(1, reach // 2 + 1)
    for m in later:
        pl.when(s // 2 + m < ns // 2)(functools.partial(send_x, m))
    x_sends = [x_copy(0, 1)] + [x_copy(m, r) for m in later for r in range(2)]

    def send_row(j, _):
        copy_to(row_buf.at[s], row_buf.at[s], s_row, r_row.at[zo], j, c).start()
        return 0

    def send_row_inner(j, _):
        return send_row(zo * INNER + lax.rem(yc + j, INNER), 0)

    def rows_of(k, count):
        return copy_to(row_buf.at[pl.ds(0, count)], row_buf.at[pl.ds(0, count)], s_row, r_row.at[k], sib, c)

    lax.fori_loop(1, INNER, send_row_inner, 0)
    lax.fori_loop((zo + 1) * INNER, ns, send_row, 0)
    pl.when(zh == 1)(send_relays)
    for dz in range(1, zs):
        pl.when(zh + dz > zs)(functools.partial(send_chunks, dz))

    lane = lax.broadcasted_iota(jnp.int32, (quarter, width), 1)
    lane_group = lax.rem(lane, half) // per

    def answer(k, _):
        rows_of(k, INNER).wait_recv()
        return lax.fori_loop(k * INNER, (k + 1) * INNER, send_row, 0)

    lax.fori_loop(0, zo, answer, 0)
    for m in later:
        pl.when(s // 2 + m >= ns // 2)(functools.partial(send_x, m))

    def toeplitz():
        rows_of(zo, INNER - 1).wait_recv()

        def rest(k, _):
            rows_of(k, INNER).wait_recv()
            return 0

        lax.fori_loop(zo + 1, outer, rest, 0)
        for i in range(ns):
            gathered[i:i + 1, :] = row_buf[i]
        for t in range(8):
            turned = gathered[...] if t == 0 else pltpu.roll(gathered[...], LANES - t * groups, 1)
            unpacked[pl.ds(t, ns, stride=8), :] = turned
        for b in range(taps // LANES):
            frow[:, b * LANES:(b + 1) * LANES] = unpacked[b * LANES:(b + 1) * LANES, :].T[0:groups, :]

        def build(g, _):
            wide = jnp.broadcast_to(frow[pl.ds(e * mine + g, 1), :], (block, span))
            toep[g] = pltpu.roll(wide, 0, 1, stride=1, stride_axis=0).astype(bf16)
            return 0

        lax.fori_loop(0, mine, build, 0)

    own.wait()
    halo = []
    total = jnp.zeros((mine, span), f32)
    for dz in near:
        if dz == near[-1]:
            toeplitz()
        def await_chunks(dz=dz):
            for key in wanted((zs - dz) % zs):
                chunk_copy(*key).wait_recv()

        if dz == 2:
            pl.when(zh < 2)(await_chunks)
            pl.when(zh >= 2)(forward.wait_recv)
        else:
            await_chunks()
        zg = lax.rem(zh + dz, zs)
        part = (pl.ds(0, 2), pl.ds(zg * CROSS, CROSS))
        for m in range(1, reach // 2 + 1):
            halo.append(send(dy_buf.at[part], dy_buf.at[pl.ds(2 * m, 2), pl.ds(zg * CROSS, CROSS)],
                             s_halo.at[m - 1, dz], r_halo.at[m - 1, dz], lax.rem(s + ns - 2 * m, ns), c))
        if dz == 1:
            pl.when(zh + dz < zs)(functools.partial(send_chunks, dz))
            pl.when(zh == 0)(send_relays)
        elif dz == 3:
            pl.when(zh + dz < zs)(functools.partial(send_chunks, dz))
            pl.when(zh < 2)(send_forward)
        elif dz == 0:
            for copy in x_sends:
                copy.wait_recv()
            for i in range(reach + 1):
                xw[i * block:(i + 1) * block, 0:half] = x_ext[i + 1]
                xw[i * block:(i + 1) * block, half:width] = x_ext[i]
        at = pl.ds(pl.multiple_of(zg * quarter, quarter), quarter)
        for b in range(2):
            chunk = dy_buf[b, pl.ds(zg * CROSS, CROSS)].astype(f32).reshape(quarter, half).astype(bf16)
            dyc[at, b * half:(b + 1) * half] = chunk
        grads = dyc[at, :]
        masked = jnp.concatenate(
            [jnp.where(lane_group == q, grads, jnp.zeros_like(grads)) for q in range(mine)], axis=0)
        products = lax.dot_general(masked, xw[...], (((1,), (1,)), ((), ())), preferred_element_type=f32)
        sums = []
        for q in range(mine):
            skewed = pltpu.roll(products[q * quarter:(q + 1) * quarter, :], 0, 1, stride=1, stride_axis=0)
            sums.append(jnp.sum(skewed, axis=0, keepdims=True))
        total = total + pltpu.roll(jnp.concatenate(sums, axis=0), zg * quarter, 1)

    dh_rows[pl.ds(pl.multiple_of(e * mine, mine), mine), :] = pltpu.roll(total, span - (block - 1), 1)
    for b in range(taps // LANES):
        dh_cols[b * LANES:(b + 1) * LANES, :] = dh_rows[:, b * LANES:(b + 1) * LANES].T
    rows_packed = dh_cols[pl.ds(0, ns, stride=8), :]
    for t in range(1, 8):
        rows_packed = rows_packed + pltpu.roll(dh_cols[pl.ds(t, ns, stride=8), :], t * groups, 1)
    staged[...] = rows_packed
    for i in range(ns):
        packed[i] = staged[i:i + 1, :]

    def send_terms(j, _):
        peer = lax.rem(s + j, ns)
        copy_to(packed.at[peer], rs.at[j], s_rs, r_rs, peer, c).start()
        return 0

    lax.fori_loop(1, ns, send_terms, 0)
    rs[0] = packed[s]
    all_terms = copy_to(packed.at[pl.ds(0, ns - 1)], rs.at[pl.ds(1, ns - 1)], s_rs, r_rs, sib, c)

    for copy in halo:
        copy.wait_recv()
    for b in range(1, reach + 2):
        tile = dy_buf[b].astype(f32).reshape(block, half).astype(bf16)
        if b <= reach:
            dyc[b * block:(b + 1) * block, 0:half] = tile
        if b >= 2:
            dyc[(b - 1) * block:b * block, half:width] = tile

    lane_all = lax.rem(lax.broadcasted_iota(jnp.int32, (block, width), 1), half) // per

    def convolve(i, acc):
        filters = toep[pl.ds(i * GANG, GANG)].reshape(GANG * block, span)
        out = jnp.dot(filters, dyc[...], preferred_element_type=f32)
        for q in range(GANG):
            acc = jnp.where(lane_all == i * GANG + q, out[q * block:(q + 1) * block, :], acc)
        return acc

    grads_in = lax.fori_loop(0, mine // GANG, convolve, jnp.zeros((block, width), f32)).astype(bf16)
    for b in range(2):
        dx_out[b] = grads_in[:, b * half:(b + 1) * half]
    swap = send(dx_out.at[1 - e], dx_buf.at[e], s_dx, r_dx, sib, c)
    at = pl.ds(pl.multiple_of(e * half, half), half)
    kept = pltpu.make_async_copy(dx_out.at[e], dx_hbm.at[:, at], s_loc.at[2])
    kept.start()
    swap.wait_recv()
    at = pl.ds(pl.multiple_of((1 - e) * half, half), half)
    other = pltpu.make_async_copy(dx_buf.at[1 - e], dx_hbm.at[:, at], s_loc.at[3])
    other.start()

    all_terms.wait_recv()
    terms = jnp.sum(rs[...], axis=0)
    for t in range(8):
        dh_ref[t:t + 1, :] = terms[:, t * groups:(t + 1) * groups]

    kept.wait()
    other.wait()
    def await_sends(dz):
        for key in wanted(dz):
            chunk_copy(*key).wait_send()

    for dz in range(zs):
        if dz != 2:
            await_sends(dz)
    pl.when(zh >= 2)(functools.partial(await_sends, 2))

    def await_relays():
        for key in relays:
            relay_copy(*key).wait_send()
        forward.wait_send()

    pl.when(zh < 2)(await_relays)
    rows_of(zo, ns - 1).wait_send()
    for copy in [*x_sends, *halo, all_terms, swap]:
        copy.wait_send()


def on_device(ns, nc, dy, x, filt):
    rows = dy.shape[0]
    block, width = x.shape
    half = width // 2
    groups = filt.shape[1]
    taps = filt.shape[0] * ns
    reach = taps // block
    span = taps + block
    zs = nc // CROSS
    f32, bf16 = jnp.float32, jnp.bfloat16
    vmem, dma = pltpu.VMEM, pltpu.SemaphoreType.DMA
    return pl.pallas_call(
        functools.partial(kernel, ns, nc),
        out_shape=(jax.ShapeDtypeStruct(x.shape, bf16), jax.ShapeDtypeStruct(filt.shape, f32)),
        in_specs=[pl.BlockSpec(memory_space=pltpu.HBM)] * 3,
        out_specs=(pl.BlockSpec(memory_space=pl.ANY), pl.BlockSpec(memory_space=pltpu.VMEM)),
        scratch_shapes=[
            vmem(filt.shape, bf16),
            vmem((reach + 2, nc, rows, half), bf16),
            vmem((span, width), bf16),
            vmem((block, width), bf16),
            vmem((2, block, half), bf16),
            vmem((reach + 2, block, half), bf16),
            vmem((span, width), bf16),
            vmem((ns, 1, LANES), f32),
            vmem((ns, LANES), f32),
            vmem((taps, LANES), f32),
            vmem((groups, span), f32),
            vmem((groups // 2, block, span), bf16),
            vmem((LANES, span), f32),
            vmem((taps, LANES), f32),
            vmem((ns, LANES), f32),
            vmem((ns, 1, LANES), f32),
            vmem((ns, 1, LANES), f32),
            vmem((2, block, half), bf16),
            vmem((2, block, half), bf16),
            vmem((2, CROSS, rows, half), bf16),
            dma((zs, CROSS, 2)), dma((zs, CROSS, 2)),
            dma((CROSS, 2)), dma((CROSS, 2)), dma, dma,
            dma((reach // 2 + 1, 2)), dma((reach // 2 + 1, 2)),
            dma, dma((ns // INNER,)),
            dma((reach // 2, zs)), dma((reach // 2, zs)),
            dma, dma, dma, dma,
            dma((5,)),
        ],
        compiler_params=pltpu.CompilerParams(
            collective_id=0, has_side_effects=True, vmem_limit_bytes=60 * 2**20),
    )(dy, x, filt)


def solution(mesh):
    ns, nc = mesh.shape["seq"], mesh.shape["chan"]
    in_specs = (P(("seq", "chan"), None), P("seq", "chan"), P("seq", "chan"))
    out_specs = (P("seq", "chan"), P("seq", "chan"))
    return jax.shard_map(
        functools.partial(on_device, ns, nc), mesh=mesh, in_specs=in_specs, out_specs=out_specs, check_vma=False)
```

```python
import functools

import jax
import jax.numpy as jnp
from jax import lax
from jax.experimental import pallas as pl
from jax.experimental.pallas import tpu as pltpu
from jax.sharding import PartitionSpec as P

MESH = pl.DeviceIdType.MESH
LANES = 128
INNER = 8
CROSS = 4
GANG = 4


def kernel(ns, nc, dy_hbm, x_hbm, filt_hbm, dx_hbm, dh_ref,
           filt_ref, dy_buf, dyc, x_buf, x_half, x_ext, xw, row_buf, gathered, unpacked, frow, toep, dh_rows, dh_cols,
           staged, packed, rs, dx_out, relayed,
           s_a2a, r_a2a, s_rel, r_rel, s_fwd, r_fwd, s_x, r_x, s_row, r_row, s_halo, r_halo, s_rs, r_rs, s_dx, r_dx, s_loc):
    f32, bf16 = jnp.float32, jnp.bfloat16
    zs = nc // CROSS
    rows, half = dy_buf.shape[2], dy_buf.shape[3]
    block = rows * nc
    width = 2 * half
    quarter = block // zs
    span = dyc.shape[0]
    reach = span // block - 1
    taps = reach * block
    groups = filt_ref.shape[1]
    per = width // groups
    mine = groups // 2
    s, c = lax.axis_index("seq"), lax.axis_index("chan")
    e = lax.rem(s, 2)
    sib = s + 1 - 2 * e
    outer, zo, yc = ns // INNER, s // INNER, lax.rem(s, INNER)
    zh, xx = c // CROSS, lax.rem(c, CROSS)

    def chan_peer(dz, dx):
        return lax.rem(zh + dz, zs) * CROSS + lax.rem(xx + dx, CROSS)

    def copy_to(src, dst, ssem, rsem, seq, chan):
        return pltpu.make_async_remote_copy(
            src_ref=src, dst_ref=dst, send_sem=ssem, recv_sem=rsem, device_id=(seq, chan), device_id_type=MESH)

    def send(*args):
        copy = copy_to(*args)
        copy.start()
        return copy

    far = sorted(range(zs), key=lambda d: -min(d, zs - d))
    near = sorted(range(zs), key=lambda d: min(d, zs - d))
    cores = ((0, s), (1, sib))

    barrier = pltpu.get_barrier_semaphore()

    def greet_all(dz):
        for dx in range(CROSS):
            for r, seq in cores:
                if dz or dx:
                    pl.semaphore_signal(barrier, inc=1, device_id=(seq, chan_peer(dz, dx)), device_id_type=MESH)

    for dz in far[:-1]:
        pl.when(zh + dz < zs)(functools.partial(greet_all, dz))
    greet_all(0)

    def greet(j, _):
        pl.semaphore_signal(barrier, inc=1, device_id=(j, c), device_id_type=MESH)
        return 0

    def greet_inner(j, _):
        return greet(zo * INNER + lax.rem(yc + j, INNER), 0)

    lax.fori_loop(0, zo * INNER, greet, 0)
    lax.fori_loop(1, INNER, greet_inner, 0)

    x_in = pltpu.make_async_copy(x_hbm, x_buf, s_loc.at[1])
    x_in.start()
    filt_in = pltpu.make_async_copy(filt_hbm, filt_ref, s_loc.at[3])
    filt_in.start()
    own = pltpu.make_async_copy(
        dy_hbm.at[:, pl.ds(pl.multiple_of(c * width + e * half, half), half)], dy_buf.at[e, c], s_loc.at[0])
    own.start()

    pl.semaphore_wait(barrier, 2 * (CROSS - 1) + INNER - 1 + INNER * (outer - 1 - zo) + 2 * CROSS * zh)

    def chunk_copy(dz, dx, r):
        peer = chan_peer(dz, dx)
        their = e if r == 0 else 1 - e
        start = pl.multiple_of(peer * width + their * half, half)
        return copy_to(dy_hbm.at[:, pl.ds(start, half)], dy_buf.at[e, c],
                       s_a2a.at[dz, dx, r], r_a2a.at[dz, dx, r], cores[r][1], peer)

    def wanted(dz):
        return [(dz, dx, r) for dx in range(CROSS) for r in range(2) if dz or dx or r]

    def send_chunks(dz):
        for key in wanted(dz):
            chunk_copy(*key).start()

    via = lax.rem(zs + 1 - zh, zs)

    def relay_copy(dx, r):
        column = lax.rem(xx + dx, CROSS)
        their = e if r == 0 else 1 - e
        start = pl.multiple_of(((zh + 2) * CROSS + column) * width + their * half, half)
        return copy_to(dy_hbm.at[:, pl.ds(start, half)], relayed.at[e, xx],
                       s_rel.at[dx, r], r_rel.at[dx, r], cores[r][1], via * CROSS + column)

    relays = [(dx, r) for dx in range(CROSS) for r in range(2)]

    def send_relays():
        for key in relays:
            relay_copy(*key).start()

    forward = copy_to(relayed, dy_buf.at[pl.ds(0, 2), pl.ds(via * CROSS, CROSS)], s_fwd, r_fwd,
                      s, (3 - zh) * CROSS + xx)

    def send_forward():
        for key in relays:
            relay_copy(*key).wait_recv()
        forward.start()

    for dz in range(1, zs):
        pl.when(zh + dz == zs)(functools.partial(send_chunks, dz))
    send_chunks(0)

    unpacked[...] = jnp.zeros_like(unpacked)
    filt_in.wait()
    unpacked[0:8, 0:groups] = filt_ref[...].astype(f32)
    row_buf[s] = jnp.sum(pltpu.roll(unpacked[0:8, :], 0, 1, stride=groups, stride_axis=0), axis=0, keepdims=True)
    frow[...] = jnp.zeros_like(frow)
    dh_rows[...] = jnp.zeros_like(dh_rows)

    x_in.wait()
    r0 = lax.broadcasted_iota(jnp.int32, (block, block), 0)
    r1 = lax.broadcasted_iota(jnp.int32, (block, block), 1)
    flip = jnp.where(r0 + r1 == block - 1, 1.0, 0.0).astype(bf16)
    for h in range(2):
        x_half[h] = jnp.dot(flip, x_buf[:, h * half:(h + 1) * half], preferred_element_type=f32).astype(bf16)
    x_ext[1 - e] = x_half[e]

    def x_copy(m, r):
        their = e if r == 0 else 1 - e
        return copy_to(x_half.at[their], x_ext.at[2 * m + 1 - e], s_x.at[m, r], r_x.at[m, r],
                       lax.rem(cores[r][1] + 2 * m, ns), c)

    def send_x(m):
        for r in range(2):
            x_copy(m, r).start()

    x_copy(0, 1).start()
    later = range(1, reach // 2 + 1)
    for m in later:
        pl.when(s // 2 + m < ns // 2)(functools.partial(send_x, m))
    x_sends = [x_copy(0, 1)] + [x_copy(m, r) for m in later for r in range(2)]

    def send_row(j, _):
        copy_to(row_buf.at[s], row_buf.at[s], s_row, r_row.at[zo], j, c).start()
        return 0

    def send_row_inner(j, _):
        return send_row(zo * INNER + lax.rem(yc + j, INNER), 0)

    def rows_of(k, count):
        return copy_to(row_buf.at[pl.ds(0, count)], row_buf.at[pl.ds(0, count)], s_row, r_row.at[k], sib, c)

    lax.fori_loop(1, INNER, send_row_inner, 0)
    lax.fori_loop((zo + 1) * INNER, ns, send_row, 0)
    pl.when(zh == 1)(send_relays)
    for dz in range(1, zs):
        pl.when(zh + dz > zs)(functools.partial(send_chunks, dz))

    lane = lax.broadcasted_iota(jnp.int32, (quarter, width), 1)
    lane_group = lax.rem(lane, half) // per

    def answer(k, _):
        rows_of(k, INNER).wait_recv()
        return lax.fori_loop(k * INNER, (k + 1) * INNER, send_row, 0)

    lax.fori_loop(0, zo, answer, 0)
    for m in later:
        pl.when(s // 2 + m >= ns // 2)(functools.partial(send_x, m))

    def toeplitz():
        rows_of(zo, INNER - 1).wait_recv()

        def rest(k, _):
            rows_of(k, INNER).wait_recv()
            return 0

        lax.fori_loop(zo + 1, outer, rest, 0)
        for i in range(ns):
            gathered[i:i + 1, :] = row_buf[i]
        for t in range(8):
            turned = gathered[...] if t == 0 else pltpu.roll(gathered[...], LANES - t * groups, 1)
            unpacked[pl.ds(t, ns, stride=8), :] = turned
        for b in range(taps // LANES):
            frow[:, b * LANES:(b + 1) * LANES] = unpacked[b * LANES:(b + 1) * LANES, :].T[0:groups, :]

        def build(g, _):
            wide = jnp.broadcast_to(frow[pl.ds(e * mine + g, 1), :], (block, span))
            toep[g] = pltpu.roll(wide, 0, 1, stride=1, stride_axis=0).astype(bf16)
            return 0

        lax.fori_loop(0, mine, build, 0)

    own.wait()
    halo = []
    total = jnp.zeros((mine, span), f32)
    for dz in near:
        if dz == near[-1]:
            toeplitz()
        def await_chunks(dz=dz):
            for key in wanted((zs - dz) % zs):
                chunk_copy(*key).wait_recv()

        if dz == 2:
            pl.when(zh < 2)(await_chunks)
            pl.when(zh >= 2)(forward.wait_recv)
        else:
            await_chunks()
        zg = lax.rem(zh + dz, zs)
        part = (pl.ds(0, 2), pl.ds(zg * CROSS, CROSS))
        for m in range(1, reach // 2 + 1):
            halo.append(send(dy_buf.at[part], dy_buf.at[pl.ds(2 * m, 2), pl.ds(zg * CROSS, CROSS)],
                             s_halo.at[m - 1, dz], r_halo.at[m - 1, dz], lax.rem(s + ns - 2 * m, ns), c))
        if dz == 1:
            pl.when(zh + dz < zs)(functools.partial(send_chunks, dz))
            pl.when(zh == 0)(send_relays)
        elif dz == 3:
            pl.when(zh + dz < zs)(functools.partial(send_chunks, dz))
            pl.when(zh < 2)(send_forward)
        elif dz == 0:
            for copy in x_sends:
                copy.wait_recv()
            for i in range(reach + 1):
                xw[i * block:(i + 1) * block, 0:half] = x_ext[i + 1]
                xw[i * block:(i + 1) * block, half:width] = x_ext[i]
        at = pl.ds(pl.multiple_of(zg * quarter, quarter), quarter)
        for b in range(2):
            chunk = dy_buf[b, pl.ds(zg * CROSS, CROSS)].astype(f32).reshape(quarter, half).astype(bf16)
            dyc[at, b * half:(b + 1) * half] = chunk
        grads = dyc[at, :]
        masked = jnp.concatenate(
            [jnp.where(lane_group == q, grads, jnp.zeros_like(grads)) for q in range(mine)], axis=0)
        products = lax.dot_general(masked, xw[...], (((1,), (1,)), ((), ())), preferred_element_type=f32)
        sums = []
        for q in range(mine):
            skewed = pltpu.roll(products[q * quarter:(q + 1) * quarter, :], 0, 1, stride=1, stride_axis=0)
            sums.append(jnp.sum(skewed, axis=0, keepdims=True))
        total = total + pltpu.roll(jnp.concatenate(sums, axis=0), zg * quarter, 1)

    dh_rows[pl.ds(pl.multiple_of(e * mine, mine), mine), :] = pltpu.roll(total, span - (block - 1), 1)
    for b in range(taps // LANES):
        dh_cols[b * LANES:(b + 1) * LANES, :] = dh_rows[:, b * LANES:(b + 1) * LANES].T
    rows_packed = dh_cols[pl.ds(0, ns, stride=8), :]
    for t in range(1, 8):
        rows_packed = rows_packed + pltpu.roll(dh_cols[pl.ds(t, ns, stride=8), :], t * groups, 1)
    staged[...] = rows_packed
    for i in range(ns):
        packed[i] = staged[i:i + 1, :]

    def send_terms(j, _):
        peer = lax.rem(s + j, ns)
        copy_to(packed.at[peer], rs.at[j], s_rs, r_rs, peer, c).start()
        return 0

    lax.fori_loop(1, ns, send_terms, 0)
    rs[0] = packed[s]
    all_terms = copy_to(packed.at[pl.ds(0, ns - 1)], rs.at[pl.ds(1, ns - 1)], s_rs, r_rs, sib, c)

    for copy in halo:
        copy.wait_recv()
    for b in range(1, reach + 2):
        tile = dy_buf[b].astype(f32).reshape(block, half).astype(bf16)
        if b <= reach:
            dyc[b * block:(b + 1) * block, 0:half] = tile
        if b >= 2:
            dyc[(b - 1) * block:b * block, half:width] = tile

    lane_all = lax.rem(lax.broadcasted_iota(jnp.int32, (block, width), 1), half) // per

    def convolve(i, acc):
        filters = toep[pl.ds(i * GANG, GANG)].reshape(GANG * block, span)
        out = jnp.dot(filters, dyc[...], preferred_element_type=f32)
        for q in range(GANG):
            acc = jnp.where(lane_all == i * GANG + q, out[q * block:(q + 1) * block, :], acc)
        return acc

    grads_in = lax.fori_loop(0, mine // GANG, convolve, jnp.zeros((block, width), f32)).astype(bf16)
    for b in range(2):
        dx_out[b] = grads_in[:, b * half:(b + 1) * half]
    at = pl.ds(pl.multiple_of(e * half, half), half)
    swap = send(dx_out.at[1 - e], dx_hbm.at[:, at], s_dx, r_dx, sib, c)
    kept = pltpu.make_async_copy(dx_out.at[e], dx_hbm.at[:, at], s_loc.at[2])
    kept.start()

    all_terms.wait_recv()
    terms = jnp.sum(rs[...], axis=0)
    for t in range(8):
        dh_ref[t:t + 1, :] = terms[:, t * groups:(t + 1) * groups]

    kept.wait()
    swap.wait_recv()
    def await_sends(dz):
        for key in wanted(dz):
            chunk_copy(*key).wait_send()

    for dz in range(zs):
        if dz != 2:
            await_sends(dz)
    pl.when(zh >= 2)(functools.partial(await_sends, 2))

    def await_relays():
        for key in relays:
            relay_copy(*key).wait_send()
        forward.wait_send()

    pl.when(zh < 2)(await_relays)
    rows_of(zo, ns - 1).wait_send()
    for copy in [*x_sends, *halo, all_terms, swap]:
        copy.wait_send()


def on_device(ns, nc, dy, x, filt):
    rows = dy.shape[0]
    block, width = x.shape
    half = width // 2
    groups = filt.shape[1]
    taps = filt.shape[0] * ns
    reach = taps // block
    span = taps + block
    zs = nc // CROSS
    f32, bf16 = jnp.float32, jnp.bfloat16
    vmem, dma = pltpu.VMEM, pltpu.SemaphoreType.DMA
    return pl.pallas_call(
        functools.partial(kernel, ns, nc),
        out_shape=(jax.ShapeDtypeStruct(x.shape, bf16), jax.ShapeDtypeStruct(filt.shape, f32)),
        in_specs=[pl.BlockSpec(memory_space=pltpu.HBM)] * 3,
        out_specs=(pl.BlockSpec(memory_space=pl.ANY), pl.BlockSpec(memory_space=pltpu.VMEM)),
        scratch_shapes=[
            vmem(filt.shape, bf16),
            vmem((reach + 2, nc, rows, half), bf16),
            vmem((span, width), bf16),
            vmem((block, width), bf16),
            vmem((2, block, half), bf16),
            vmem((reach + 2, block, half), bf16),
            vmem((span, width), bf16),
            vmem((ns, 1, LANES), f32),
            vmem((ns, LANES), f32),
            vmem((taps, LANES), f32),
            vmem((groups, span), f32),
            vmem((groups // 2, block, span), bf16),
            vmem((LANES, span), f32),
            vmem((taps, LANES), f32),
            vmem((ns, LANES), f32),
            vmem((ns, 1, LANES), f32),
            vmem((ns, 1, LANES), f32),
            vmem((2, block, half), bf16),
            vmem((2, CROSS, rows, half), bf16),
            dma((zs, CROSS, 2)), dma((zs, CROSS, 2)),
            dma((CROSS, 2)), dma((CROSS, 2)), dma, dma,
            dma((reach // 2 + 1, 2)), dma((reach // 2 + 1, 2)),
            dma, dma((ns // INNER,)),
            dma((reach // 2, zs)), dma((reach // 2, zs)),
            dma, dma, dma, dma,
            dma((4,)),
        ],
        compiler_params=pltpu.CompilerParams(
            collective_id=0, has_side_effects=True, vmem_limit_bytes=40 * 2**20),
    )(*(pltpu.with_memory_space_constraint(a, pltpu.HBM) for a in (dy, x, filt)))


def solution(mesh):
    ns, nc = mesh.shape["seq"], mesh.shape["chan"]
    in_specs = (P(("seq", "chan"), None), P("seq", "chan"), P("seq", "chan"))
    out_specs = (P("seq", "chan"), P("seq", "chan"))
    return jax.shard_map(
        functools.partial(on_device, ns, nc), mesh=mesh, in_specs=in_specs, out_specs=out_specs, check_vma=False)
```

```python
import functools

import jax
import jax.numpy as jnp
from jax import lax
from jax.experimental import pallas as pl
from jax.experimental.pallas import tpu as pltpu
from jax.sharding import PartitionSpec as P

MESH = pl.DeviceIdType.MESH
LANES = 128
INNER = 8
CROSS = 4
GANG = 4


def kernel(ns, nc, dy_hbm, x_hbm, filt_hbm, dx_hbm, dh_ref,
           filt_ref, dy_buf, dyc, x_buf, x_half, x_ext, xw, row_buf, gathered, unpacked, frow, toep, dh_rows, dh_cols,
           staged, packed, rs, dx_out, relayed,
           s_a2a, r_a2a, s_rel, r_rel, s_fwd, r_fwd, s_x, r_x, s_row, r_row, s_halo, r_halo, s_rs, r_rs, s_dx, r_dx, s_loc):
    f32, bf16 = jnp.float32, jnp.bfloat16
    zs = nc // CROSS
    rows, half = dy_buf.shape[2], dy_buf.shape[3]
    block = rows * nc
    width = 2 * half
    quarter = block // zs
    span = dyc.shape[0]
    reach = span // block - 1
    taps = reach * block
    groups = filt_ref.shape[1]
    per = width // groups
    mine = groups // 2
    s, c = lax.axis_index("seq"), lax.axis_index("chan")
    e = lax.rem(s, 2)
    sib = s + 1 - 2 * e
    outer, zo, yc = ns // INNER, s // INNER, lax.rem(s, INNER)
    zh, xx = c // CROSS, lax.rem(c, CROSS)

    def chan_peer(dz, dx):
        return lax.rem(zh + dz, zs) * CROSS + lax.rem(xx + dx, CROSS)

    def copy_to(src, dst, ssem, rsem, seq, chan):
        return pltpu.make_async_remote_copy(
            src_ref=src, dst_ref=dst, send_sem=ssem, recv_sem=rsem, device_id=(seq, chan), device_id_type=MESH)

    def send(*args):
        copy = copy_to(*args)
        copy.start()
        return copy

    far = sorted(range(zs), key=lambda d: -min(d, zs - d))
    near = sorted(range(zs), key=lambda d: min(d, zs - d))
    cores = ((0, s), (1, sib))

    barrier = pltpu.get_barrier_semaphore()

    def greet_all(dz):
        for dx in range(CROSS):
            for r, seq in cores:
                if dz or dx:
                    pl.semaphore_signal(barrier, inc=1, device_id=(seq, chan_peer(dz, dx)), device_id_type=MESH)

    for dz in far[:-1]:
        pl.when(zh + dz < zs)(functools.partial(greet_all, dz))
    greet_all(0)

    def greet(j, _):
        pl.semaphore_signal(barrier, inc=1, device_id=(j, c), device_id_type=MESH)
        return 0

    def greet_inner(j, _):
        return greet(zo * INNER + lax.rem(yc + j, INNER), 0)

    lax.fori_loop(0, zo * INNER, greet, 0)
    lax.fori_loop(1, INNER, greet_inner, 0)

    x_in = pltpu.make_async_copy(x_hbm, x_buf, s_loc.at[1])
    x_in.start()
    filt_in = pltpu.make_async_copy(filt_hbm, filt_ref, s_loc.at[3])
    filt_in.start()
    own = pltpu.make_async_copy(
        dy_hbm.at[:, pl.ds(pl.multiple_of(c * width + e * half, half), half)], dy_buf.at[e, c], s_loc.at[0])
    own.start()

    pl.semaphore_wait(barrier, 2 * (CROSS - 1) + INNER - 1 + INNER * (outer - 1 - zo) + 2 * CROSS * zh)

    def chunk_copy(dz, dx, r):
        peer = chan_peer(dz, dx)
        their = e if r == 0 else 1 - e
        start = pl.multiple_of(peer * width + their * half, half)
        return copy_to(dy_hbm.at[:, pl.ds(start, half)], dy_buf.at[e, c],
                       s_a2a.at[dz, dx, r], r_a2a.at[dz, dx, r], cores[r][1], peer)

    def wanted(dz):
        return [(dz, dx, r) for dx in range(CROSS) for r in range(2) if dz or dx or r]

    def send_chunks(dz):
        for key in wanted(dz):
            chunk_copy(*key).start()

    via = lax.rem(zs + 1 - zh, zs)

    def relay_copy(dx, r):
        column = lax.rem(xx + dx, CROSS)
        their = e if r == 0 else 1 - e
        start = pl.multiple_of(((zh + 2) * CROSS + column) * width + their * half, half)
        return copy_to(dy_hbm.at[:, pl.ds(start, half)], relayed.at[e, xx],
                       s_rel.at[dx, r], r_rel.at[dx, r], cores[r][1], via * CROSS + column)

    relays = [(dx, r) for dx in range(CROSS) for r in range(2)]

    def send_relays():
        for key in relays:
            relay_copy(*key).start()

    forward = copy_to(relayed, dy_buf.at[pl.ds(0, 2), pl.ds(via * CROSS, CROSS)], s_fwd, r_fwd,
                      s, (3 - zh) * CROSS + xx)

    def send_forward():
        for key in relays:
            relay_copy(*key).wait_recv()
        forward.start()

    for dz in range(1, zs):
        pl.when(zh + dz == zs)(functools.partial(send_chunks, dz))
    send_chunks(0)

    unpacked[...] = jnp.zeros_like(unpacked)
    filt_in.wait()
    unpacked[0:8, 0:groups] = filt_ref[...].astype(f32)
    row_buf[s] = jnp.sum(pltpu.roll(unpacked[0:8, :], 0, 1, stride=groups, stride_axis=0), axis=0, keepdims=True)
    frow[...] = jnp.zeros_like(frow)
    dh_rows[...] = jnp.zeros_like(dh_rows)

    x_in.wait()
    r0 = lax.broadcasted_iota(jnp.int32, (block, block), 0)
    r1 = lax.broadcasted_iota(jnp.int32, (block, block), 1)
    flip = jnp.where(r0 + r1 == block - 1, 1.0, 0.0).astype(bf16)
    for h in range(2):
        x_half[h] = jnp.dot(flip, x_buf[:, h * half:(h + 1) * half], preferred_element_type=f32).astype(bf16)
    x_ext[1 - e] = x_half[e]

    def x_copy(m, r):
        their = e if r == 0 else 1 - e
        return copy_to(x_half.at[their], x_ext.at[2 * m + 1 - e], s_x.at[m, r], r_x.at[m, r],
                       lax.rem(cores[r][1] + 2 * m, ns), c)

    def send_x(m):
        for r in range(2):
            x_copy(m, r).start()

    x_copy(0, 1).start()
    later = range(1, reach // 2 + 1)
    for m in later:
        pl.when(s // 2 + m < ns // 2)(functools.partial(send_x, m))
    x_sends = [x_copy(0, 1)] + [x_copy(m, r) for m in later for r in range(2)]

    def send_row(j, _):
        copy_to(row_buf.at[s], row_buf.at[s], s_row, r_row.at[zo], j, c).start()
        return 0

    def send_row_inner(j, _):
        return send_row(zo * INNER + lax.rem(yc + j, INNER), 0)

    def rows_of(k, count):
        return copy_to(row_buf.at[pl.ds(0, count)], row_buf.at[pl.ds(0, count)], s_row, r_row.at[k], sib, c)

    lax.fori_loop(1, INNER, send_row_inner, 0)
    lax.fori_loop((zo + 1) * INNER, ns, send_row, 0)
    pl.when(zh == 1)(send_relays)
    for dz in range(1, zs):
        pl.when(zh + dz > zs)(functools.partial(send_chunks, dz))

    lane = lax.broadcasted_iota(jnp.int32, (quarter, width), 1)
    lane_group = lax.rem(lane, half) // per

    def answer(k, _):
        rows_of(k, INNER).wait_recv()
        return lax.fori_loop(k * INNER, (k + 1) * INNER, send_row, 0)

    lax.fori_loop(0, zo, answer, 0)
    for m in later:
        pl.when(s // 2 + m >= ns // 2)(functools.partial(send_x, m))

    def toeplitz():
        rows_of(zo, INNER - 1).wait_recv()

        def rest(k, _):
            rows_of(k, INNER).wait_recv()
            return 0

        lax.fori_loop(zo + 1, outer, rest, 0)
        for i in range(ns):
            gathered[i:i + 1, :] = row_buf[i]
        for t in range(8):
            turned = gathered[...] if t == 0 else pltpu.roll(gathered[...], LANES - t * groups, 1)
            unpacked[pl.ds(t, ns, stride=8), :] = turned
        for b in range(taps // LANES):
            frow[:, b * LANES:(b + 1) * LANES] = unpacked[b * LANES:(b + 1) * LANES, :].T[0:groups, :]

        def build(g, _):
            wide = jnp.broadcast_to(frow[pl.ds(e * mine + g, 1), :], (block, span))
            toep[g] = pltpu.roll(wide, 0, 1, stride=1, stride_axis=0).astype(bf16)
            return 0

        lax.fori_loop(0, mine, build, 0)

    own.wait()
    halo = []
    total = jnp.zeros((mine, span), f32)
    for dz in near:
        if dz == near[-1]:
            toeplitz()
        def await_chunks(dz=dz):
            for key in wanted((zs - dz) % zs):
                chunk_copy(*key).wait_recv()

        if dz == 2:
            pl.when(zh < 2)(await_chunks)
            pl.when(zh >= 2)(forward.wait_recv)
        else:
            await_chunks()
        zg = lax.rem(zh + dz, zs)
        part = (pl.ds(0, 2), pl.ds(zg * CROSS, CROSS))
        for m in range(1, reach // 2 + 1):
            halo.append(send(dy_buf.at[part], dy_buf.at[pl.ds(2 * m, 2), pl.ds(zg * CROSS, CROSS)],
                             s_halo.at[m - 1, dz], r_halo.at[m - 1, dz], lax.rem(s + ns - 2 * m, ns), c))
        if dz == 1:
            pl.when(zh + dz < zs)(functools.partial(send_chunks, dz))
            pl.when(zh == 0)(send_relays)
        elif dz == 3:
            pl.when(zh + dz < zs)(functools.partial(send_chunks, dz))
            pl.when(zh < 2)(send_forward)
        elif dz == 0:
            for copy in x_sends:
                copy.wait_recv()
            for i in range(reach + 1):
                xw[i * block:(i + 1) * block, 0:half] = x_ext[i + 1]
                xw[i * block:(i + 1) * block, half:width] = x_ext[i]
        at = pl.ds(pl.multiple_of(zg * quarter, quarter), quarter)
        for b in range(2):
            chunk = dy_buf[b, pl.ds(zg * CROSS, CROSS)].astype(f32).reshape(quarter, half).astype(bf16)
            dyc[at, b * half:(b + 1) * half] = chunk
        grads = dyc[at, :]
        masked = jnp.concatenate(
            [jnp.where(lane_group == q, grads, jnp.zeros_like(grads)) for q in range(mine)], axis=0)
        products = lax.dot_general(masked, xw[...], (((1,), (1,)), ((), ())), preferred_element_type=f32)
        sums = []
        for q in range(mine):
            skewed = pltpu.roll(products[q * quarter:(q + 1) * quarter, :], 0, 1, stride=1, stride_axis=0)
            sums.append(jnp.sum(skewed, axis=0, keepdims=True))
        total = total + pltpu.roll(jnp.concatenate(sums, axis=0), zg * quarter, 1)

    dh_rows[pl.ds(pl.multiple_of(e * mine, mine), mine), :] = pltpu.roll(total, span - (block - 1), 1)
    for b in range(taps // LANES):
        dh_cols[b * LANES:(b + 1) * LANES, :] = dh_rows[:, b * LANES:(b + 1) * LANES].T
    rows_packed = dh_cols[pl.ds(0, ns, stride=8), :]
    for t in range(1, 8):
        rows_packed = rows_packed + pltpu.roll(dh_cols[pl.ds(t, ns, stride=8), :], t * groups, 1)
    staged[...] = rows_packed
    for i in range(ns):
        packed[i] = staged[i:i + 1, :]

    def send_terms(i, _):
        for u in range(INNER - 1):
            j = 1 + i * (INNER - 1) + u
            peer = lax.rem(s + j, ns)
            copy_to(packed.at[peer], rs.at[j], s_rs, r_rs, peer, c).start()
        return 0

    lax.fori_loop(0, (ns - 1) // (INNER - 1), send_terms, 0)
    rs[0] = packed[s]
    all_terms = copy_to(packed.at[pl.ds(0, ns - 1)], rs.at[pl.ds(1, ns - 1)], s_rs, r_rs, sib, c)

    for copy in halo:
        copy.wait_recv()
    for b in range(1, reach + 2):
        tile = dy_buf[b].astype(f32).reshape(block, half).astype(bf16)
        if b <= reach:
            dyc[b * block:(b + 1) * block, 0:half] = tile
        if b >= 2:
            dyc[(b - 1) * block:b * block, half:width] = tile

    lane_all = lax.rem(lax.broadcasted_iota(jnp.int32, (block, width), 1), half) // per

    def convolve(i, acc):
        filters = toep[pl.ds(i * GANG, GANG)].reshape(GANG * block, span)
        out = jnp.dot(filters, dyc[...], preferred_element_type=f32)
        for q in range(GANG):
            acc = jnp.where(lane_all == i * GANG + q, out[q * block:(q + 1) * block, :], acc)
        return acc

    grads_in = lax.fori_loop(0, mine // GANG, convolve, jnp.zeros((block, width), f32)).astype(bf16)
    for b in range(2):
        dx_out[b] = grads_in[:, b * half:(b + 1) * half]
    at = pl.ds(pl.multiple_of(e * half, half), half)
    swap = send(dx_out.at[1 - e], dx_hbm.at[:, at], s_dx, r_dx, sib, c)
    kept = pltpu.make_async_copy(dx_out.at[e], dx_hbm.at[:, at], s_loc.at[2])
    kept.start()

    all_terms.wait_recv()
    terms = jnp.sum(rs[...], axis=0)
    for t in range(8):
        dh_ref[t:t + 1, :] = terms[:, t * groups:(t + 1) * groups]

    kept.wait()
    swap.wait_recv()
    def await_sends(dz):
        for key in wanted(dz):
            chunk_copy(*key).wait_send()

    for dz in range(zs):
        if dz != 2:
            await_sends(dz)
    pl.when(zh >= 2)(functools.partial(await_sends, 2))

    def await_relays():
        for key in relays:
            relay_copy(*key).wait_send()
        forward.wait_send()

    pl.when(zh < 2)(await_relays)
    rows_of(zo, ns - 1).wait_send()
    for copy in [*x_sends, *halo, all_terms, swap]:
        copy.wait_send()


def on_device(ns, nc, dy, x, filt):
    rows = dy.shape[0]
    block, width = x.shape
    half = width // 2
    groups = filt.shape[1]
    taps = filt.shape[0] * ns
    reach = taps // block
    span = taps + block
    zs = nc // CROSS
    f32, bf16 = jnp.float32, jnp.bfloat16
    vmem, dma = pltpu.VMEM, pltpu.SemaphoreType.DMA
    return pl.pallas_call(
        functools.partial(kernel, ns, nc),
        out_shape=(jax.ShapeDtypeStruct(x.shape, bf16), jax.ShapeDtypeStruct(filt.shape, f32)),
        in_specs=[pl.BlockSpec(memory_space=pltpu.HBM)] * 3,
        out_specs=(pl.BlockSpec(memory_space=pl.ANY), pl.BlockSpec(memory_space=pltpu.VMEM)),
        scratch_shapes=[
            vmem(filt.shape, bf16),
            vmem((reach + 2, nc, rows, half), bf16),
            vmem((span, width), bf16),
            vmem((block, width), bf16),
            vmem((2, block, half), bf16),
            vmem((reach + 2, block, half), bf16),
            vmem((span, width), bf16),
            vmem((ns, 1, LANES), f32),
            vmem((ns, LANES), f32),
            vmem((taps, LANES), f32),
            vmem((groups, span), f32),
            vmem((groups // 2, block, span), bf16),
            vmem((LANES, span), f32),
            vmem((taps, LANES), f32),
            vmem((ns, LANES), f32),
            vmem((ns, 1, LANES), f32),
            vmem((ns, 1, LANES), f32),
            vmem((2, block, half), bf16),
            vmem((2, CROSS, rows, half), bf16),
            dma((zs, CROSS, 2)), dma((zs, CROSS, 2)),
            dma((CROSS, 2)), dma((CROSS, 2)), dma, dma,
            dma((reach // 2 + 1, 2)), dma((reach // 2 + 1, 2)),
            dma, dma((ns // INNER,)),
            dma((reach // 2, zs)), dma((reach // 2, zs)),
            dma, dma, dma, dma,
            dma((4,)),
        ],
        compiler_params=pltpu.CompilerParams(
            collective_id=0, has_side_effects=True, vmem_limit_bytes=40 * 2**20),
    )(*(pltpu.with_memory_space_constraint(a, pltpu.HBM) for a in (dy, x, filt)))


def solution(mesh):
    ns, nc = mesh.shape["seq"], mesh.shape["chan"]
    in_specs = (P(("seq", "chan"), None), P("seq", "chan"), P("seq", "chan"))
    out_specs = (P("seq", "chan"), P("seq", "chan"))
    return jax.shard_map(
        functools.partial(on_device, ns, nc), mesh=mesh, in_specs=in_specs, out_specs=out_specs, check_vma=False)
```
